256 devices in a mesh: expert: 8 (over z), dp: 32 (over y, x, core).
Axes of the slice: x: 4, y: 4, z: 8, core: 2. Of those that a mesh axis runs over, the one named last changes fastest.
Arguments:
- row_acts: bfloat16 [8, 32768, 2048], P('expert', 'dp'), may hold values from -6 to 6
- row_grads: bfloat16 [8, 32768, 768], P('expert', 'dp'), may hold values from -6 to 6
- grad_factor: bfloat16 [8, 768, 768], P('expert', None, 'dp'), may hold values from -0.21875 to 0.21875
- value_factor: bfloat16 [8, 2048, 768], P('expert', None, 'dp'), may hold values from -0.125 to 0.125
- counts: int32 [8, 32], P('expert', 'dp'), may hold values from 128 to 1024, as said below
- row_token: int32 [8, 32768], P('expert', 'dp'), may hold values from 0 to 2047, as said below
Outputs:
- influence: float32 [65536, 24], P(('expert', 'dp'))
The draws below stay inside these ranges and needn't reach their ends.
Inputs may be any that keep to these rules, and one draw needn't show every extreme that they name: counts[e, b] slots at the start of each block of 1024 slots are live; some block has all 1024 live. `row_token`: within one block of 1024 slots of one expert the ids are distinct, dead slots included.
All inputs are finite; a program needn't handle non-finite values.
Results may differ from the reference program's by a relative error of at most 0.0003.
Values may be sent and summed in bfloat16 or wider, within the bound.
No kernel may reach another device: no remote copies, remote signals or barrier semaphores. Data moves between devices by JAX's collectives and lax.ppermute only.
A program may use at most 64 MiB of HBM per device.

```python
import jax
import jax.numpy as jnp
from jax import lax

MODEL = 2048
MOE_FF = 768
RANK = 32
QUERIES = 24
CAP = 1024
TOK_DEV = 256
EXPERTS = 8
ROWS = 32768
TOKENS = 65536


def draw_counts(key, part):
    nblocks = ROWS // CAP
    level_key = jax.random.fold_in(key, 11)
    jitter_key = jax.random.fold_in(key, 12)
    row_key = jax.random.fold_in(key, 13)
    column_key = jax.random.fold_in(key, 14)
    level = jax.random.randint(level_key, (EXPERTS, 1), CAP // 8, CAP + 1)
    jitter = jax.random.randint(jitter_key, (EXPERTS, nblocks), 0, CAP // 4 + 1)
    filled = jnp.minimum(level + jitter, CAP)
    chosen_row = jax.random.randint(row_key, (), 0, EXPERTS)
    chosen_column = jax.random.randint(column_key, (), 0, nblocks)
    row_grid = jnp.arange(EXPERTS, dtype=jnp.int32)[:, None]
    column_grid = jnp.arange(nblocks, dtype=jnp.int32)[None, :]
    marked = (row_grid == chosen_row) & (column_grid == chosen_column)
    return jnp.where(marked, CAP, filled).astype(jnp.int32)


def draw_row_token(key, part):
    nblocks = ROWS // CAP
    shard_tokens = TOK_DEV * EXPERTS
    block_keys = jax.random.split(jax.random.fold_in(key, 21), EXPERTS * nblocks)

    def one_block(block_key):
        return jax.random.permutation(block_key, shard_tokens)[:CAP]
    owner_ids = jax.vmap(one_block)(block_keys)
    return owner_ids.reshape(EXPERTS, ROWS).astype(jnp.int32)


def shard_levels(stream_key, dims, pieces, low, high):
    level, own = 1.0, jax.random.fold_in(stream_key, 6)
    for position, parts in pieces:
        draws = jnp.exp(jax.random.uniform(jax.random.fold_in(own, position), (parts,), jnp.float32, low / len(pieces), high / len(pieces)))
        level = level * jnp.repeat(draws, dims[position] // parts).reshape([-1 if axis == position else 1 for axis in range(len(dims))])
    return level


def normal_values(key, shape, spread, limit, pieces=(), kind=jnp.bfloat16):
    values = jax.random.normal(key, shape, jnp.float32) * spread
    if len(pieces) > 0:
        values = shard_levels(key, shape, pieces, -0.22, 0.18) * values
    return jnp.clip(values, min=-limit, max=limit).astype(kind)


def setup_inputs(seed: int = 0) -> dict:
    seeds = jax.random.split(jax.random.key(seed), 7)
    row_acts = normal_values(seeds[0], (EXPERTS, ROWS, MODEL), 1.0, 6.0, ((0, 8), (1, 32)))
    row_grads = normal_values(seeds[1], (EXPERTS, ROWS, MOE_FF), 1.0, 6.0, ((0, 8), (1, 32)))
    grad_factor = normal_values(seeds[2], (EXPERTS, MOE_FF, QUERIES * RANK), MOE_FF ** -0.5, 0.21875, ((0, 8), (2, 32)))
    value_factor = normal_values(seeds[3], (EXPERTS, MODEL, QUERIES * RANK), MODEL ** -0.5, 0.125, ((0, 8), (2, 32)))
    counts = draw_counts(jax.random.fold_in(seeds[6], 71), 0)
    row_token = draw_row_token(jax.random.fold_in(seeds[6], 71), 0)
    return dict(row_acts=row_acts, row_grads=row_grads, grad_factor=grad_factor, value_factor=value_factor, counts=counts, row_token=row_token)


epsilon = 1e-06

def reference(row_acts, row_grads, grad_factor, value_factor, counts, row_token):
    nblocks = ROWS // CAP
    shard_tokens = TOK_DEV * EXPERTS
    column_ids = jnp.arange(QUERIES * RANK, dtype=jnp.int32)[:, None] // RANK
    query_ids = jnp.arange(QUERIES, dtype=jnp.int32)[None, :]
    grouping = (column_ids == query_ids).astype(jnp.float32)
    slot_ids = jnp.arange(CAP, dtype=jnp.int32)

    def one_block(block_id):

        def one_expert(carry, expert_id):
            total_now, norm_now = carry
            start = (block_id * CAP).astype(jnp.int32)
            activ = lax.dynamic_slice(row_acts, (expert_id, start, jnp.int32(0)), (1, CAP, MODEL))[0]
            gradient = lax.dynamic_slice(row_grads, (expert_id, start, jnp.int32(0)), (1, CAP, MOE_FF))[0]
            acts_proj = jnp.dot(activ, value_factor[expert_id], preferred_element_type=jnp.float32)
            grads_proj = jnp.dot(gradient, grad_factor[expert_id], preferred_element_type=jnp.float32)
            scores = jnp.dot(acts_proj * grads_proj, grouping, precision=lax.Precision.HIGHEST)
            live = (slot_ids < counts[expert_id, block_id]).astype(jnp.float32)
            norms = lax.optimization_barrier(jnp.sum(jnp.square(activ.astype(jnp.float32)), 1)) * lax.optimization_barrier(jnp.sum(jnp.square(gradient.astype(jnp.float32)), 1))
            owner_ids = lax.dynamic_slice(row_token, (expert_id, start), (1, CAP))[0]
            total_now = total_now.at[owner_ids].add(scores * live[:, None])
            norm_now = norm_now.at[owner_ids].add(norms * live)
            return ((total_now, norm_now), None)
        start_carry = (jnp.zeros((shard_tokens, QUERIES), jnp.float32), jnp.zeros((shard_tokens,), jnp.float32))
        (total_now, norm_now), _ = lax.scan(one_expert, start_carry, jnp.arange(EXPERTS, dtype=jnp.int32))
        return (total_now, norm_now)
    totals, norm_sum = lax.map(one_block, jnp.arange(nblocks, dtype=jnp.int32))
    factor = lax.rsqrt(norm_sum / (MODEL * MOE_FF) + epsilon) / jnp.sqrt(jnp.float32(RANK))
    result = totals * factor[..., None]
    result = result.reshape(nblocks, EXPERTS, TOK_DEV, QUERIES).transpose(1, 0, 2, 3)
    return result.reshape(TOKENS, QUERIES)
```

```python
import jax
import jax.numpy as jnp
from jax import lax
from jax.sharding import PartitionSpec as P

MODEL = 2048
MOE_FF = 768
RANK = 32
QUERIES = 24
TOK_DEV = 256
SIDE = 4
OFFSETS = (0, -1, 1, 2)

epsilon = 1e-06


def place(y, x, core):
    return ((y % SIDE) * SIDE + x % SIDE) * 2 + core


def pairs(step):
    return [
        (place(y, x, core), place(*step(y, x, core)))
        for y in range(SIDE)
        for x in range(SIDE)
        for core in range(2)
    ]


def first_axis(shift):
    return pairs(lambda y, x, core: (y, x + shift, 0) if core == 0 else (y + shift, x, 1))


def second_axis(shift):
    return pairs(lambda y, x, core: (y + shift, x, 0) if core == 0 else (y, x + shift, 1))


SIBLING = pairs(lambda y, x, core: (y, x, 1 - core))


def slot_queries(per_device):
    me = lax.axis_index("dp")
    my_core, my_x, my_y = me % 2, (me // 2) % SIDE, me // (2 * SIDE)
    offsets = jnp.array(OFFSETS, jnp.int32)
    second = offsets[:, None, None, None]
    core = jnp.stack([my_core, 1 - my_core])[None, :, None, None]
    first = offsets[None, None, :, None]
    x = (my_x + jnp.where(core == 0, first, second)) % SIDE
    y = (my_y + jnp.where(core == 0, second, first)) % SIDE
    lane = lax.broadcasted_iota(jnp.int32, (1, 1, 1, per_device), 3)
    column = ((y * SIDE + x) * 2 + core) * per_device + lane
    return column.reshape(-1) // RANK


def gather(shard):
    send = lambda value, table: lax.ppermute(value, "dp", table)
    line = [shard] + [send(shard, first_axis(-d)) for d in OFFSETS[1:]]
    line = jnp.concatenate(line, 0)
    mine = [line] + [send(line, second_axis(-d)) for d in OFFSETS[1:]]
    theirs = [send(block, SIBLING) for block in mine]
    return jnp.concatenate([block for pair in zip(mine, theirs) for block in pair], 0)


def local(row_acts, row_grads, grad_factor, value_factor, counts, row_token):
    activ = row_acts[0]
    gradient = row_grads[0]
    shard = jnp.concatenate([value_factor[0].T, grad_factor[0].T], 1)
    factors = gather(shard)
    contract = (((1,), (1,)), ((), ()))
    acts_proj = lax.dot_general(
        factors[:, :MODEL], activ, contract, preferred_element_type=jnp.float32
    )
    grads_proj = lax.dot_general(
        factors[:, MODEL:], gradient, contract, preferred_element_type=jnp.float32
    )
    queries = slot_queries(shard.shape[0])
    query_ids = lax.broadcasted_iota(jnp.int32, (QUERIES, queries.shape[0]), 0)
    grouping = (query_ids == queries[None, :]).astype(jnp.float32)
    scores = jnp.dot(grouping, acts_proj * grads_proj, precision=lax.Precision.HIGHEST)
    slots = activ.shape[0]
    live = lax.broadcasted_iota(jnp.int32, (slots,), 0) < counts[0, 0]
    norms = jnp.sum(jnp.square(activ.astype(jnp.float32)), 1) * jnp.sum(
        jnp.square(gradient.astype(jnp.float32)), 1
    )
    experts = lax.axis_size("expert")
    shard_tokens = TOK_DEV * experts
    owner_grid = lax.broadcasted_iota(jnp.int32, (slots, shard_tokens), 1)
    onehot = ((row_token[0][:, None] == owner_grid) & live[:, None]).astype(jnp.float32)
    table = jnp.concatenate([scores, norms[None, :]], 0)
    dense = jnp.dot(table, onehot, precision=lax.Precision.HIGHEST)
    dense = dense.reshape(QUERIES + 1, experts, TOK_DEV).transpose(1, 0, 2)
    summed = lax.all_to_all(dense, "expert", 0, 0).sum(0)
    totals, norm_sum = summed[:QUERIES], summed[QUERIES]
    factor = lax.rsqrt(norm_sum / (MODEL * MOE_FF) + epsilon) / jnp.sqrt(jnp.float32(RANK))
    return (totals * factor[None, :]).T


def solution(mesh):
    return jax.shard_map(
        local,
        mesh=mesh,
        in_specs=(
            P("expert", "dp", None),
            P("expert", "dp", None),
            P("expert", None, "dp"),
            P("expert", None, "dp"),
            P("expert", "dp"),
            P("expert", "dp"),
        ),
        out_specs=P(("expert", "dp"), None),
        check_vma=False,
    )
```

```python
import functools

import jax
import jax.numpy as jnp
from jax import lax
from jax.experimental import pallas as pl
from jax.experimental.pallas import tpu as pltpu
from jax.sharding import PartitionSpec as P

MODEL = 2048
MOE_FF = 768
RANK = 32
QUERIES = 24
TOK_DEV = 256
SIDE = 4
OFFSETS = (0, -1, 1, 2)
ROW_TILE = 256

epsilon = 1e-06

CONTRACT_LAST = (((1,), (1,)), ((), ()))
VMEM = pl.BlockSpec(memory_space=pltpu.VMEM)


def place(y, x, core):
    return ((y % SIDE) * SIDE + x % SIDE) * 2 + core


def pairs(step):
    return [
        (place(y, x, core), place(*step(y, x, core)))
        for y in range(SIDE)
        for x in range(SIDE)
        for core in range(2)
    ]


def first_axis(shift):
    return pairs(lambda y, x, core: (y, x + shift, 0) if core == 0 else (y + shift, x, 1))


def second_axis(shift):
    return pairs(lambda y, x, core: (y + shift, x, 0) if core == 0 else (y, x + shift, 1))


SIBLING = pairs(lambda y, x, core: (y, x, 1 - core))


def send(value, table):
    return lax.ppermute(value, "dp", table)


def slot_queries(per_device):
    me = lax.axis_index("dp")
    core, my_x, my_y = me % 2, (me // 2) % SIDE, me // (2 * SIDE)
    slots = SIDE * SIDE * per_device
    slot = lax.broadcasted_iota(jnp.int32, (QUERIES, slots), 1)
    piece = slot // per_device
    offset = lambda i: jnp.where(i == 1, SIDE - 1, jnp.where(i == 0, 0, i - 1))
    first, second = offset(piece % SIDE), offset(piece // SIDE)
    x = (my_x + jnp.where(core == 0, first, second)) % SIDE
    y = (my_y + jnp.where(core == 0, second, first)) % SIDE
    column = ((y * SIDE + x) * 2 + core) * per_device + slot % per_device
    return column // RANK


def split(value, terms):
    parts = []
    for _ in range(terms):
        part = value.astype(jnp.bfloat16)
        parts.append(part)
        value = value - part.astype(jnp.float32)
    return parts


def scores_kernel(acts, grads, w0, w1, w2, w3, grouping, out, factors):
    width = w0.shape[0]
    for i, w in enumerate((w0, w1, w2, w3)):
        factors[i * width : (i + 1) * width, :] = w[...]
    dot = functools.partial(
        lax.dot_general, dimension_numbers=CONTRACT_LAST, preferred_element_type=jnp.float32
    )
    for start in range(0, acts.shape[0], ROW_TILE):
        rows = slice(start, start + ROW_TILE)
        product = dot(factors[:, :MODEL], acts[rows, :]) * dot(factors[:, MODEL:], grads[rows, :])
        high, low = split(product, 2)
        out[:, rows] = jnp.dot(
            grouping[...], high, preferred_element_type=jnp.float32
        ) + jnp.dot(grouping[...], low, preferred_element_type=jnp.float32)


def row_scores(acts, grads, pieces, grouping):
    rows = acts.shape[0]
    slots = 4 * pieces[0].shape[0]
    return pl.pallas_call(
        scores_kernel,
        out_shape=jax.ShapeDtypeStruct((QUERIES, rows), jnp.float32),
        in_specs=[VMEM] * 7,
        out_specs=VMEM,
        scratch_shapes=[pltpu.VMEM((slots, MODEL + MOE_FF), jnp.bfloat16)],
        compiler_params=pltpu.CompilerParams(vmem_limit_bytes=24 << 20),
        cost_estimate=pl.CostEstimate(
            flops=2 * rows * slots * (MODEL + MOE_FF), bytes_accessed=8 << 20, transcendentals=0
        ),
        name="row_scores",
    )(acts, grads, *pieces, grouping)


def owners_kernel(tokens, norms, onehot, dense):
    owner = lax.broadcasted_iota(jnp.int32, (TOK_DEV, tokens.shape[1]), 0)
    high, middle, low = split(norms[...], 3)
    for start in range(0, onehot.shape[0], TOK_DEV):
        hot = (owner + start == tokens[...]).astype(jnp.float32).astype(jnp.bfloat16)
        onehot[start : start + TOK_DEV, :] = hot
        part = [
            lax.dot_general(
                jnp.broadcast_to(term, (8, term.shape[1])),
                hot,
                CONTRACT_LAST,
                preferred_element_type=jnp.float32,
            )
            for term in (high, middle, low)
        ]
        dense[:, start : start + TOK_DEV] = part[0] + part[1] + part[2]


def owners(tokens, norms, shard_tokens):
    rows = tokens.shape[1]
    return pl.pallas_call(
        owners_kernel,
        out_shape=(
            jax.ShapeDtypeStruct((shard_tokens, rows), jnp.bfloat16),
            jax.ShapeDtypeStruct((8, shard_tokens), jnp.float32),
        ),
        in_specs=[VMEM] * 2,
        out_specs=(VMEM, VMEM),
        compiler_params=pltpu.CompilerParams(vmem_limit_bytes=16 << 20),
        cost_estimate=pl.CostEstimate(
            flops=2 * rows * shard_tokens * 128, bytes_accessed=8 << 20, transcendentals=0
        ),
        name="owners",
    )(tokens, norms)


def scatter_kernel(mine, theirs, onehot, dense_norm, out):
    table = jnp.concatenate(split(mine[...] + theirs[...], 3), 0)
    for i in range(out.shape[0]):
        owned = slice(i * TOK_DEV, (i + 1) * TOK_DEV)
        part = lax.dot_general(
            table, onehot[owned, :], CONTRACT_LAST, preferred_element_type=jnp.float32
        )
        out[i, :QUERIES, :] = (
            part[:QUERIES] + part[QUERIES : 2 * QUERIES] + part[2 * QUERIES :]
        )
        out[i, QUERIES:, :] = dense_norm[:1, owned]


def scatter(mine, theirs, onehot, dense_norm):
    shard_tokens = onehot.shape[0]
    return pl.pallas_call(
        scatter_kernel,
        out_shape=jax.ShapeDtypeStruct(
            (shard_tokens // TOK_DEV, QUERIES + 1, TOK_DEV), jnp.float32
        ),
        in_specs=[VMEM] * 4,
        out_specs=VMEM,
        compiler_params=pltpu.CompilerParams(vmem_limit_bytes=16 << 20),
        name="scatter",
    )(mine, theirs, onehot, dense_norm)


def local(row_acts, row_grads, grad_factor, value_factor, counts, row_token):
    acts, grads = row_acts[0], row_grads[0]
    experts = lax.axis_size("expert")
    shard = jnp.concatenate([value_factor[0].T, grad_factor[0].T], 1)
    line = [shard] + [send(shard, first_axis(-d)) for d in OFFSETS[1:]]
    their_acts, their_grads = send(acts, SIBLING), send(grads, SIBLING)
    line = jnp.concatenate(line, 0)
    line, late_acts, late_grads, tokens = lax.optimization_barrier((line, acts, grads, row_token))
    pieces = [line] + [send(line, second_axis(-d)) for d in OFFSETS[1:]]
    slots = acts.shape[0]
    live = lax.broadcasted_iota(jnp.int32, (1, slots), 1) < counts[0, 0]
    norms = jnp.sum(jnp.square(late_acts.astype(jnp.float32)), 1) * jnp.sum(
        jnp.square(late_grads.astype(jnp.float32)), 1
    )
    onehot, dense_norm = owners(
        jnp.where(live, tokens, -1), norms[None, :], TOK_DEV * experts
    )
    queries = slot_queries(shard.shape[0])
    query_ids = lax.broadcasted_iota(jnp.int32, queries.shape, 0)
    grouping = (query_ids == queries).astype(jnp.bfloat16)
    for_them = row_scores(their_acts, their_grads, pieces, grouping)
    theirs = send(for_them, SIBLING)
    mine = row_scores(acts, grads, pieces, grouping)
    dense = scatter(mine, theirs, onehot, dense_norm)
    summed = lax.all_to_all(dense, "expert", 0, 0).sum(0)
    totals, norm_sum = summed[:QUERIES], summed[QUERIES]
    factor = lax.rsqrt(norm_sum / (MODEL * MOE_FF) + epsilon) / jnp.sqrt(jnp.float32(RANK))
    return (totals * factor[None, :]).T


def solution(mesh):
    return jax.shard_map(
        local,
        mesh=mesh,
        in_specs=(
            P("expert", "dp", None),
            P("expert", "dp", None),
            P("expert", None, "dp"),
            P("expert", None, "dp"),
            P("expert", "dp"),
            P("expert", "dp"),
        ),
        out_specs=P(("expert", "dp"), None),
        check_vma=False,
    )
```

```python
import functools

import jax
import jax.numpy as jnp
from jax import lax
from jax.experimental import pallas as pl
from jax.experimental.pallas import tpu as pltpu
from jax.sharding import PartitionSpec as P

MODEL = 2048
MOE_FF = 768
RANK = 32
QUERIES = 24
TOK_DEV = 256
SIDE = 4
OFFSETS = (0, -1, 1, 2)
HALF = TOK_DEV // 2

epsilon = 1e-06

CONTRACT_LAST = (((1,), (1,)), ((), ()))
VMEM = pl.BlockSpec(memory_space=pltpu.VMEM)


def place(y, x, core):
    return ((y % SIDE) * SIDE + x % SIDE) * 2 + core


def pairs(step):
    return [
        (place(y, x, core), place(*step(y, x, core)))
        for y in range(SIDE)
        for x in range(SIDE)
        for core in range(2)
    ]


def first_axis(shift):
    return pairs(lambda y, x, core: (y, x + shift, 0) if core == 0 else (y + shift, x, 1))


def second_axis(shift):
    return pairs(lambda y, x, core: (y + shift, x, 0) if core == 0 else (y, x + shift, 1))


SIBLING = pairs(lambda y, x, core: (y, x, 1 - core))


def send(value, table):
    return lax.ppermute(value, "dp", table)


def slot_queries(per_device):
    me = lax.axis_index("dp")
    core, my_x, my_y = me & 1, (me >> 1) & (SIDE - 1), me >> 3
    slots = SIDE * SIDE * per_device
    slot = lax.broadcasted_iota(jnp.int32, (QUERIES, slots), 1)
    piece = (slot * (65536 // per_device + 1)) >> 16
    offset = lambda i: jnp.where(i == 1, SIDE - 1, jnp.where(i == 0, 0, i - 1))
    first, second = offset(piece & (SIDE - 1)), offset(piece >> 2)
    swapped = (first - second) * core
    x = (my_x + first - swapped) & (SIDE - 1)
    y = (my_y + second + swapped) & (SIDE - 1)
    column = ((y * SIDE + x) * 2 + core) * per_device + slot - piece * per_device
    return column >> 5


def split(value, terms):
    parts = []
    for _ in range(terms):
        part = value.astype(jnp.bfloat16)
        parts.append(part)
        value = value - part.astype(jnp.float32)
    return parts


def line_kernel(own, before, after, across, out):
    width = own.shape[0]
    for i, shard in enumerate((own, before, after, across)):
        out[i * width : (i + 1) * width, :] = shard[...]


def join(shards):
    width, depth = shards[0].shape
    return pl.pallas_call(
        line_kernel,
        out_shape=jax.ShapeDtypeStruct((len(shards) * width, depth), shards[0].dtype),
        in_specs=[VMEM] * len(shards),
        out_specs=VMEM,
        compiler_params=pltpu.CompilerParams(vmem_limit_bytes=1 << 20),
        name="line",
    )(*shards)


def scores_kernel(acts, grads, w0, w1, w2, w3, grouping, out, factors):
    width = w0.shape[0]
    for i, w in enumerate((w0, w1, w2, w3)):
        factors[i * width : (i + 1) * width, :] = w[...]
    dot = functools.partial(
        lax.dot_general, dimension_numbers=CONTRACT_LAST, preferred_element_type=jnp.float32
    )
    product = dot(factors[:, :MODEL], acts[...]) * dot(factors[:, MODEL:], grads[...])
    high, low = split(product, 2)
    out[...] = jnp.dot(grouping[...], high, preferred_element_type=jnp.float32) + jnp.dot(
        grouping[...], low, preferred_element_type=jnp.float32
    )


def row_scores(acts, grads, pieces, grouping):
    rows = acts.shape[0]
    slots = 4 * pieces[0].shape[0]
    return pl.pallas_call(
        scores_kernel,
        out_shape=jax.ShapeDtypeStruct((QUERIES, rows), jnp.float32),
        in_specs=[VMEM] * 7,
        out_specs=VMEM,
        scratch_shapes=[pltpu.VMEM((slots, MODEL + MOE_FF), jnp.bfloat16)],
        compiler_params=pltpu.CompilerParams(vmem_limit_bytes=4 << 20),
        cost_estimate=pl.CostEstimate(
            flops=2 * rows * slots * (MODEL + MOE_FF), bytes_accessed=8 << 20, transcendentals=0
        ),
        name="row_scores",
    )(acts, grads, *pieces, grouping)


def owners_kernel(tokens, norms, onehot, dense, grouping):
    queries = slot_queries(grouping.shape[1] // (SIDE * SIDE))
    query_ids = lax.broadcasted_iota(jnp.int32, queries.shape, 0)
    grouping[...] = (query_ids == queries).astype(jnp.float32).astype(jnp.bfloat16)
    owner = lax.broadcasted_iota(jnp.int32, (TOK_DEV, tokens.shape[1]), 0)
    high, middle, low = split(norms[...], 3)
    for start in range(0, onehot.shape[0], TOK_DEV):
        hot = (owner + start == tokens[...]).astype(jnp.float32).astype(jnp.bfloat16)
        onehot[start : start + TOK_DEV, :] = hot
        part = [
            lax.dot_general(
                jnp.broadcast_to(term, (8, term.shape[1])),
                hot,
                CONTRACT_LAST,
                preferred_element_type=jnp.float32,
            )
            for term in (high, middle, low)
        ]
        dense[:, start : start + TOK_DEV] = part[0] + part[1] + part[2]


def owners(tokens, norms, shard_tokens, slots):
    rows = tokens.shape[1]
    return pl.pallas_call(
        owners_kernel,
        out_shape=(
            jax.ShapeDtypeStruct((shard_tokens, rows), jnp.bfloat16),
            jax.ShapeDtypeStruct((8, shard_tokens), jnp.float32),
            jax.ShapeDtypeStruct((QUERIES, slots), jnp.bfloat16),
        ),
        in_specs=[VMEM] * 2,
        out_specs=(VMEM, VMEM, VMEM),
        compiler_params=pltpu.CompilerParams(vmem_limit_bytes=3 << 20),
        cost_estimate=pl.CostEstimate(
            flops=2 * rows * shard_tokens * 128, bytes_accessed=8 << 20, transcendentals=0
        ),
        name="owners",
    )(tokens, norms)


def scatter_kernel(mine, theirs, onehot, dense_norm, out):
    table = jnp.concatenate(split(mine[...] + theirs[...], 3), 0)
    for i in range(out.shape[0]):
        owned = slice(i * TOK_DEV, (i + 1) * TOK_DEV)
        part = lax.dot_general(
            table, onehot[owned, :], CONTRACT_LAST, preferred_element_type=jnp.float32
        )
        part = part[:QUERIES] + part[QUERIES : 2 * QUERIES] + part[2 * QUERIES :]
        for half in range(2):
            lanes = slice(half * HALF, (half + 1) * HALF)
            out[i, half * QUERIES : (half + 1) * QUERIES, :] = part[:, lanes]
            out[i, 2 * QUERIES + half : 2 * QUERIES + half + 1, :] = dense_norm[
                :1, i * TOK_DEV + half * HALF : i * TOK_DEV + (half + 1) * HALF
            ]


def scatter(mine, theirs, onehot, dense_norm):
    shard_tokens = onehot.shape[0]
    return pl.pallas_call(
        scatter_kernel,
        out_shape=jax.ShapeDtypeStruct(
            (shard_tokens // TOK_DEV, 2 * QUERIES + 2, HALF), jnp.float32
        ),
        in_specs=[VMEM] * 4,
        out_specs=VMEM,
        compiler_params=pltpu.CompilerParams(vmem_limit_bytes=2 << 20),
        name="scatter",
    )(mine, theirs, onehot, dense_norm)


def local(row_acts, row_grads, grad_factor, value_factor, counts, row_token):
    acts, grads = row_acts[0], row_grads[0]
    experts = lax.axis_size("expert")
    shard = jnp.concatenate([value_factor[0].T, grad_factor[0].T], 1)
    line = [shard] + [send(shard, first_axis(-d)) for d in OFFSETS[1:]]
    their_acts, their_grads = send(acts, SIBLING), send(grads, SIBLING)
    line = join(line)
    line, tokens = lax.optimization_barrier((line, row_token))
    pieces = [line] + [send(line, second_axis(-d)) for d in OFFSETS[1:]]
    slots = acts.shape[0]
    live = lax.broadcasted_iota(jnp.int32, (1, slots), 1) < counts[0, 0]
    norms = jnp.sum(jnp.square(acts.astype(jnp.float32)), 1) * jnp.sum(
        jnp.square(grads.astype(jnp.float32)), 1
    )
    onehot, dense_norm, grouping = owners(
        jnp.where(live, tokens, -1),
        norms[None, :],
        TOK_DEV * experts,
        SIDE * SIDE * shard.shape[0],
    )
    for_them = row_scores(their_acts, their_grads, pieces, grouping)
    theirs = send(for_them, SIBLING)
    mine = row_scores(acts, grads, pieces, grouping)
    dense = scatter(mine, theirs, onehot, dense_norm)
    summed = lax.all_to_all(dense, "expert", 0, 0).sum(0)
    totals, norm_sum = summed[: 2 * QUERIES].reshape(2, QUERIES, HALF), summed[2 * QUERIES :]
    factor = lax.rsqrt(norm_sum / (MODEL * MOE_FF) + epsilon) / jnp.sqrt(jnp.float32(RANK))
    return (totals * factor[:, None, :]).transpose(0, 2, 1).reshape(TOK_DEV, QUERIES)


def solution(mesh):
    return jax.shard_map(
        local,
        mesh=mesh,
        in_specs=(
            P("expert", "dp", None),
            P("expert", "dp", None),
            P("expert", None, "dp"),
            P("expert", None, "dp"),
            P("expert", "dp"),
            P("expert", "dp"),
        ),
        out_specs=P(("expert", "dp"), None),
        check_vma=False,
    )
```

```python
import functools

import jax
import jax.numpy as jnp
from jax import lax
from jax.experimental import pallas as pl
from jax.experimental.pallas import tpu as pltpu
from jax.sharding import PartitionSpec as P

MODEL = 2048
MOE_FF = 768
RANK = 32
QUERIES = 24
TOK_DEV = 256
SIDE = 4
FIRST = (0, -1, 1, 2)
SECOND = (0, 2, -1, 1)
HALF = TOK_DEV // 2

epsilon = 1e-06

CONTRACT_LAST = (((1,), (1,)), ((), ()))
VMEM = pl.BlockSpec(memory_space=pltpu.VMEM)


def place(y, x, core):
    return ((y % SIDE) * SIDE + x % SIDE) * 2 + core


def pairs(step):
    return [
        (place(y, x, core), place(*step(y, x, core)))
        for y in range(SIDE)
        for x in range(SIDE)
        for core in range(2)
    ]


def first_axis(shift):
    return pairs(lambda y, x, core: (y, x + shift, 0) if core == 0 else (y + shift, x, 1))


def second_axis(shift):
    return pairs(lambda y, x, core: (y + shift, x, 0) if core == 0 else (y, x + shift, 1))


SIBLING = pairs(lambda y, x, core: (y, x, 1 - core))


def send(value, table):
    return lax.ppermute(value, "dp", table)


def offset(index, table):
    value = jnp.full_like(index, table[-1])
    for i, shift in enumerate(table[:-1]):
        value = jnp.where(index == i, shift, value)
    return value


def slot_queries(shape, start):
    per_device = shape[1] // (2 * SIDE)
    me = lax.axis_index("dp")
    core, my_x, my_y = me & 1, (me >> 1) & (SIDE - 1), me >> 3
    slot = lax.broadcasted_iota(jnp.int32, shape, 1) + start * SIDE * per_device
    piece = (slot * (65536 // per_device + 1)) >> 16
    first, second = offset(piece & (SIDE - 1), FIRST), offset(piece >> 2, SECOND)
    swapped = (first - second) * core
    x = (my_x + first - swapped) & (SIDE - 1)
    y = (my_y + second + swapped) & (SIDE - 1)
    column = ((y * SIDE + x) * 2 + core) * per_device + slot - piece * per_device
    return column >> 5


def split(value, terms):
    parts = []
    for _ in range(terms):
        part = value.astype(jnp.bfloat16)
        parts.append(part)
        value = value - part.astype(jnp.float32)
    return parts


def line_kernel(own, before, after, across, out):
    width = own.shape[0]
    for i, shard in enumerate((own, before, after, across)):
        out[i * width : (i + 1) * width, :] = shard[...]


def join(shards):
    width, depth = shards[0].shape
    return pl.pallas_call(
        line_kernel,
        out_shape=jax.ShapeDtypeStruct((len(shards) * width, depth), shards[0].dtype),
        in_specs=[VMEM] * len(shards),
        out_specs=VMEM,
        compiler_params=pltpu.CompilerParams(vmem_limit_bytes=1 << 20),
        name="line",
    )(*shards)


def scores_kernel(acts, grads, w0, w1, grouping, *rest):
    *base, out, factors = rest
    width = w0.shape[0]
    factors[:width, :] = w0[...]
    factors[width:, :] = w1[...]
    dot = functools.partial(
        lax.dot_general, dimension_numbers=CONTRACT_LAST, preferred_element_type=jnp.float32
    )
    product = dot(factors[:, :MODEL], acts[...]) * dot(factors[:, MODEL:], grads[...])
    high, low = split(product, 2)
    scores = jnp.dot(grouping[...], high, preferred_element_type=jnp.float32) + jnp.dot(
        grouping[...], low, preferred_element_type=jnp.float32
    )
    out[...] = scores + base[0][...] if base else scores


def row_scores(acts, grads, pieces, grouping, *base):
    rows = acts.shape[0]
    slots = 2 * pieces[0].shape[0]
    return pl.pallas_call(
        scores_kernel,
        out_shape=jax.ShapeDtypeStruct((QUERIES, rows), jnp.float32),
        in_specs=[VMEM] * (5 + len(base)),
        out_specs=VMEM,
        scratch_shapes=[pltpu.VMEM((slots, MODEL + MOE_FF), jnp.bfloat16)],
        compiler_params=pltpu.CompilerParams(vmem_limit_bytes=4 << 20),
        cost_estimate=pl.CostEstimate(
            flops=2 * rows * slots * (MODEL + MOE_FF), bytes_accessed=7 << 20, transcendentals=0
        ),
        name="late_scores" if base else "early_scores",
    )(acts, grads, *pieces, grouping, *base)


def owners_kernel(tokens, norms, onehot, dense, early, late):
    for i, grouping in enumerate((early, late)):
        queries = slot_queries(grouping.shape, 2 * i)
        query_ids = lax.broadcasted_iota(jnp.int32, grouping.shape, 0)
        grouping[...] = (query_ids == queries).astype(jnp.float32).astype(jnp.bfloat16)
    owner = lax.broadcasted_iota(jnp.int32, (TOK_DEV, tokens.shape[1]), 0)
    row = lax.broadcasted_iota(jnp.int32, (8, tokens.shape[1]), 0)
    high, middle, low = split(norms[...], 3)
    terms = jnp.where(row == 0, high, jnp.where(row == 1, middle, low))
    for start in range(0, onehot.shape[0], TOK_DEV):
        hot = (owner + start == tokens[...]).astype(jnp.float32).astype(jnp.bfloat16)
        onehot[start : start + TOK_DEV, :] = hot
        part = lax.dot_general(
            terms, hot, CONTRACT_LAST, preferred_element_type=jnp.float32
        )
        dense[:, start : start + TOK_DEV] = part[:1] + part[1:2] + part[2:3]


def owners(tokens, norms, shard_tokens, slots):
    rows = tokens.shape[1]
    return pl.pallas_call(
        owners_kernel,
        out_shape=(
            jax.ShapeDtypeStruct((shard_tokens, rows), jnp.bfloat16),
            jax.ShapeDtypeStruct((1, shard_tokens), jnp.float32),
            jax.ShapeDtypeStruct((QUERIES, slots // 2), jnp.bfloat16),
            jax.ShapeDtypeStruct((QUERIES, slots // 2), jnp.bfloat16),
        ),
        in_specs=[VMEM] * 2,
        out_specs=(VMEM,) * 4,
        compiler_params=pltpu.CompilerParams(vmem_limit_bytes=3 << 20),
        cost_estimate=pl.CostEstimate(
            flops=2 * rows * shard_tokens * 128, bytes_accessed=8 << 20, transcendentals=0
        ),
        name="owners",
    )(tokens, norms)


def scatter_kernel(mine, theirs, onehot, dense_norm, out):
    table = jnp.concatenate(split(mine[...] + theirs[...], 3), 0)
    for i in range(out.shape[0]):
        owned = slice(i * TOK_DEV, (i + 1) * TOK_DEV)
        part = lax.dot_general(
            table, onehot[owned, :], CONTRACT_LAST, preferred_element_type=jnp.float32
        )
        part = part[:QUERIES] + part[QUERIES : 2 * QUERIES] + part[2 * QUERIES :]
        for half in range(2):
            lanes = slice(half * HALF, (half + 1) * HALF)
            out[i, half * QUERIES : (half + 1) * QUERIES, :] = part[:, lanes]
            out[i, 2 * QUERIES + half : 2 * QUERIES + half + 1, :] = dense_norm[
                :, i * TOK_DEV + half * HALF : i * TOK_DEV + (half + 1) * HALF
            ]


def scatter(mine, theirs, onehot, dense_norm):
    shard_tokens = onehot.shape[0]
    return pl.pallas_call(
        scatter_kernel,
        out_shape=jax.ShapeDtypeStruct(
            (shard_tokens // TOK_DEV, 2 * QUERIES + 2, HALF), jnp.float32
        ),
        in_specs=[VMEM] * 4,
        out_specs=VMEM,
        compiler_params=pltpu.CompilerParams(vmem_limit_bytes=2 << 20),
        name="scatter",
    )(mine, theirs, onehot, dense_norm)


def local(row_acts, row_grads, grad_factor, value_factor, counts, row_token):
    acts, grads = row_acts[0], row_grads[0]
    experts = lax.axis_size("expert")
    shard = jnp.concatenate([value_factor[0].T, grad_factor[0].T], 1)
    line = [shard] + [send(shard, first_axis(-d)) for d in FIRST[1:]]
    their_acts, their_grads = send(acts, SIBLING), send(grads, SIBLING)
    norms = jnp.sum(jnp.square(acts.astype(jnp.float32)), 1) * jnp.sum(
        jnp.square(grads.astype(jnp.float32)), 1
    )
    line[-1], norms = lax.optimization_barrier((line[-1], norms))
    line = join(line)
    line, tokens = lax.optimization_barrier((line, row_token))
    pieces = [line] + [send(line, second_axis(-d)) for d in SECOND[1:]]
    slots = acts.shape[0]
    live = lax.broadcasted_iota(jnp.int32, (1, slots), 1) < counts[0, 0]
    onehot, dense_norm, early, late = owners(
        jnp.where(live, tokens, -1),
        norms[None, :],
        TOK_DEV * experts,
        SIDE * SIDE * shard.shape[0],
    )
    for_them = row_scores(their_acts, their_grads, pieces[:2], early)
    mine = row_scores(acts, grads, pieces[:2], early)
    for_them = row_scores(their_acts, their_grads, pieces[2:], late, for_them)
    theirs = send(for_them, SIBLING)
    mine = row_scores(acts, grads, pieces[2:], late, mine)
    dense = scatter(mine, theirs, onehot, dense_norm)
    summed = lax.all_to_all(dense, "expert", 0, 0).sum(0)
    totals, norm_sum = summed[: 2 * QUERIES].reshape(2, QUERIES, HALF), summed[2 * QUERIES :]
    factor = lax.rsqrt(norm_sum / (MODEL * MOE_FF) + epsilon) / jnp.sqrt(jnp.float32(RANK))
    return (totals * factor[:, None, :]).transpose(0, 2, 1).reshape(TOK_DEV, QUERIES)


def solution(mesh):
    return jax.shard_map(
        local,
        mesh=mesh,
        in_specs=(
            P("expert", "dp", None),
            P("expert", "dp", None),
            P("expert", None, "dp"),
            P("expert", None, "dp"),
            P("expert", "dp"),
            P("expert", "dp"),
        ),
        out_specs=P(("expert", "dp"), None),
        check_vma=False,
    )
```

```python
import functools

import jax
import jax.numpy as jnp
from jax import lax
from jax.experimental import pallas as pl
from jax.experimental.pallas import tpu as pltpu
from jax.sharding import PartitionSpec as P

MODEL = 2048
MOE_FF = 768
RANK = 32
QUERIES = 24
TOK_DEV = 256
SIDE = 4
FIRST = (0, -1, 1, 2)
SECOND = (0, 2, -1, 1)
HALF = TOK_DEV // 2

epsilon = 1e-06

VMEM = pl.BlockSpec(memory_space=pltpu.VMEM)


def place(y, x, core):
    return ((y % SIDE) * SIDE + x % SIDE) * 2 + core


def pairs(step):
    return [
        (place(y, x, core), place(*step(y, x, core)))
        for y in range(SIDE)
        for x in range(SIDE)
        for core in range(2)
    ]


def first_axis(shift):
    return pairs(lambda y, x, core: (y, x + shift, 0) if core == 0 else (y + shift, x, 1))


def second_axis(shift):
    return pairs(lambda y, x, core: (y + shift, x, 0) if core == 0 else (y, x + shift, 1))


SIBLING = pairs(lambda y, x, core: (y, x, 1 - core))


def send(value, table):
    return lax.ppermute(value, "dp", table)


def offset(index, table):
    value = jnp.full_like(index, table[-1])
    for i, shift in enumerate(table[:-1]):
        value = jnp.where(index == i, shift, value)
    return value


def slot_queries(shape, start):
    per_device = shape[1] // (2 * SIDE)
    me = lax.axis_index("dp")
    core, my_x, my_y = me & 1, (me >> 1) & (SIDE - 1), me >> 3
    slot = lax.broadcasted_iota(jnp.int32, shape, 1) + start * SIDE * per_device
    piece = (slot * (65536 // per_device + 1)) >> 16
    first, second = offset(piece & (SIDE - 1), FIRST), offset(piece >> 2, SECOND)
    swapped = (first - second) * core
    x = (my_x + first - swapped) & (SIDE - 1)
    y = (my_y + second + swapped) & (SIDE - 1)
    column = ((y * SIDE + x) * 2 + core) * per_device + slot - piece * per_device
    return column >> 5


def split(value, terms):
    parts = []
    for _ in range(terms):
        part = value.astype(jnp.bfloat16)
        parts.append(part)
        value = value - part.astype(jnp.float32)
    return parts


def line_kernel(own, before, after, across, out):
    width = own.shape[0]
    for i, shard in enumerate((own, before, after, across)):
        out[i * width : (i + 1) * width, :] = shard[...]


def join(shards):
    width, depth = shards[0].shape
    return pl.pallas_call(
        line_kernel,
        out_shape=jax.ShapeDtypeStruct((len(shards) * width, depth), shards[0].dtype),
        in_specs=[VMEM] * len(shards),
        out_specs=VMEM,
        compiler_params=pltpu.CompilerParams(vmem_limit_bytes=1 << 20),
        name="line",
    )(*shards)


def turn_kernel(acts, grads, acts_out, grads_out):
    for rows, turned in ((acts, acts_out), (grads, grads_out)):
        for start in range(0, rows.shape[1], TOK_DEV):
            turned[start : start + TOK_DEV, :] = rows[:, start : start + TOK_DEV].T


def turn(acts, grads):
    return pl.pallas_call(
        turn_kernel,
        out_shape=tuple(jax.ShapeDtypeStruct(x.shape[::-1], x.dtype) for x in (acts, grads)),
        in_specs=[VMEM, VMEM],
        out_specs=(VMEM, VMEM),
        compiler_params=pltpu.CompilerParams(vmem_limit_bytes=2 << 20),
        cost_estimate=pl.CostEstimate(flops=0, bytes_accessed=6 << 20, transcendentals=0),
        name="turn",
    )(acts, grads)


def scores_kernel(acts, grads, w0, w1, grouping, *rest):
    *base, out, factors = rest
    width = w0.shape[0]
    factors[:width, :] = w0[...]
    factors[width:, :] = w1[...]
    dot = functools.partial(jnp.dot, preferred_element_type=jnp.float32)
    product = dot(factors[:, :MODEL], acts[...]) * dot(factors[:, MODEL:], grads[...])
    high, low = split(product, 2)
    scores = dot(grouping[...], high) + dot(grouping[...], low)
    out[...] = scores + base[0][...] if base else scores


def row_scores(acts, grads, pieces, grouping, *base):
    rows = acts.shape[1]
    slots = 2 * pieces[0].shape[0]
    return pl.pallas_call(
        scores_kernel,
        out_shape=jax.ShapeDtypeStruct((QUERIES, rows), jnp.float32),
        in_specs=[VMEM] * (5 + len(base)),
        out_specs=VMEM,
        scratch_shapes=[pltpu.VMEM((slots, MODEL + MOE_FF), jnp.bfloat16)],
        compiler_params=pltpu.CompilerParams(vmem_limit_bytes=4 << 20),
        cost_estimate=pl.CostEstimate(
            flops=2 * rows * slots * (MODEL + MOE_FF), bytes_accessed=7 << 20, transcendentals=0
        ),
        name="late_scores" if base else "early_scores",
    )(acts, grads, *pieces, grouping, *base)


def owners_kernel(tokens, norms, onehot, dense, early, late):
    for i, grouping in enumerate((early, late)):
        queries = slot_queries(grouping.shape, 2 * i)
        query_ids = lax.broadcasted_iota(jnp.int32, grouping.shape, 0)
        grouping[...] = (query_ids == queries).astype(jnp.float32).astype(jnp.bfloat16)
    rows = tokens.shape[1]
    token = jnp.broadcast_to(tokens[...], (HALF, rows)).T
    owner = lax.broadcasted_iota(jnp.int32, (rows, HALF), 1)
    for start in range(0, onehot.shape[1], HALF):
        hot = (token == owner + start).astype(jnp.float32).astype(jnp.bfloat16)
        onehot[:, start : start + HALF] = hot
    row = lax.broadcasted_iota(jnp.int32, (8, rows), 0)
    high, middle, low = split(norms[...], 3)
    terms = jnp.where(row == 0, high, jnp.where(row == 1, middle, low))
    part = jnp.dot(terms, onehot[...], preferred_element_type=jnp.float32)
    dense[...] = part[:1] + part[1:2] + part[2:3]


def owners(tokens, norms, shard_tokens, slots):
    rows = tokens.shape[1]
    return pl.pallas_call(
        owners_kernel,
        out_shape=(
            jax.ShapeDtypeStruct((rows, shard_tokens), jnp.bfloat16),
            jax.ShapeDtypeStruct((1, shard_tokens), jnp.float32),
            jax.ShapeDtypeStruct((QUERIES, slots // 2), jnp.bfloat16),
            jax.ShapeDtypeStruct((QUERIES, slots // 2), jnp.bfloat16),
        ),
        in_specs=[VMEM] * 2,
        out_specs=(VMEM,) * 4,
        compiler_params=pltpu.CompilerParams(vmem_limit_bytes=3 << 20),
        cost_estimate=pl.CostEstimate(
            flops=2 * rows * shard_tokens * 128, bytes_accessed=8 << 20, transcendentals=0
        ),
        name="owners",
    )(tokens, norms)


def scatter_kernel(mine, theirs, onehot, dense_norm, out):
    table = jnp.concatenate(split(mine[...] + theirs[...], 3), 0)
    part = jnp.dot(table, onehot[...], preferred_element_type=jnp.float32)
    part = part[:QUERIES] + part[QUERIES : 2 * QUERIES] + part[2 * QUERIES :]
    for i in range(out.shape[0]):
        for half in range(2):
            start = i * TOK_DEV + half * HALF
            owned = slice(start, start + HALF)
            out[i, half * QUERIES : (half + 1) * QUERIES, :] = part[:, owned]
            out[i, 2 * QUERIES + half : 2 * QUERIES + half + 1, :] = dense_norm[:, owned]


def scatter(mine, theirs, onehot, dense_norm):
    shard_tokens = onehot.shape[1]
    return pl.pallas_call(
        scatter_kernel,
        out_shape=jax.ShapeDtypeStruct(
            (shard_tokens // TOK_DEV, 2 * QUERIES + 2, HALF), jnp.float32
        ),
        in_specs=[VMEM] * 4,
        out_specs=VMEM,
        compiler_params=pltpu.CompilerParams(vmem_limit_bytes=2 << 20),
        name="scatter",
    )(mine, theirs, onehot, dense_norm)


def local(row_acts, row_grads, grad_factor, value_factor, counts, row_token):
    acts, grads = row_acts[0], row_grads[0]
    experts = lax.axis_size("expert")
    shard = jnp.concatenate([value_factor[0].T, grad_factor[0].T], 1)
    line = [shard] + [send(shard, first_axis(-d)) for d in FIRST[1:]]
    their_acts, their_grads = send(acts, SIBLING), send(grads, SIBLING)
    acts_norm = jnp.sum(jnp.square(acts.astype(jnp.float32)), 1)
    line[-1], acts_norm = lax.optimization_barrier((line[-1], acts_norm))
    line = join(line)
    line, acts, grads = lax.optimization_barrier((line, acts, grads))
    pieces = [line] + [send(line, second_axis(-d)) for d in SECOND[1:]]
    slots = acts.shape[0]
    live = lax.broadcasted_iota(jnp.int32, (1, slots), 1) < counts[0, 0]
    norms = acts_norm * jnp.sum(jnp.square(grads.astype(jnp.float32)), 1)
    their_rows = turn(their_acts, their_grads)
    my_rows = turn(acts, grads)
    norms, *their_rows = lax.optimization_barrier((norms, *their_rows))
    onehot, dense_norm, early, late = owners(
        jnp.where(live, row_token, -1),
        norms[None, :],
        TOK_DEV * experts,
        SIDE * SIDE * shard.shape[0],
    )
    for_them = row_scores(*their_rows, pieces[:2], early)
    mine = row_scores(*my_rows, pieces[:2], early)
    for_them, mine = lax.optimization_barrier((for_them, mine))
    for_them = row_scores(*their_rows, pieces[2:], late, for_them)
    theirs = send(for_them, SIBLING)
    mine = row_scores(*my_rows, pieces[2:], late, mine)
    dense = scatter(mine, theirs, onehot, dense_norm)
    summed = lax.all_to_all(dense, "expert", 0, 0).sum(0)
    totals, norm_sum = summed[: 2 * QUERIES].reshape(2, QUERIES, HALF), summed[2 * QUERIES :]
    factor = lax.rsqrt(norm_sum / (MODEL * MOE_FF) + epsilon) / jnp.sqrt(jnp.float32(RANK))
    return (totals * factor[:, None, :]).transpose(0, 2, 1).reshape(TOK_DEV, QUERIES)


def solution(mesh):
    return jax.shard_map(
        local,
        mesh=mesh,
        in_specs=(
            P("expert", "dp", None),
            P("expert", "dp", None),
            P("expert", None, "dp"),
            P("expert", None, "dp"),
            P("expert", "dp"),
            P("expert", "dp"),
        ),
        out_specs=P(("expert", "dp"), None),
        check_vma=False,
    )
```

```python
import functools

import jax
import jax.numpy as jnp
from jax import lax
from jax.experimental import pallas as pl
from jax.experimental.pallas import tpu as pltpu
from jax.sharding import PartitionSpec as P

MODEL = 2048
MOE_FF = 768
RANK = 32
QUERIES = 24
TOK_DEV = 256
SIDE = 4
FIRST = (0, -1, 1, 2)
SECOND = (0, 2, -1, 1)
STEPS = (3, 2, 1)
HALF = TOK_DEV // 2

epsilon = 1e-06

VMEM = pl.BlockSpec(memory_space=pltpu.VMEM)


def place(y, x, core):
    return ((y % SIDE) * SIDE + x % SIDE) * 2 + core


def pairs(step):
    return [
        (place(y, x, core), place(*step(y, x, core)))
        for y in range(SIDE)
        for x in range(SIDE)
        for core in range(2)
    ]


def first_axis(shift):
    return pairs(lambda y, x, core: (y, x + shift, 0) if core == 0 else (y + shift, x, 1))


def second_axis(shift):
    return pairs(lambda y, x, core: (y + shift, x, 0) if core == 0 else (y, x + shift, 1))


SIBLING = pairs(lambda y, x, core: (y, x, 1 - core))


def send(value, table):
    return lax.ppermute(value, "dp", table)


def offset(index, table):
    value = jnp.full_like(index, table[-1])
    for i, shift in enumerate(table[:-1]):
        value = jnp.where(index == i, shift, value)
    return value


def slot_queries(shape, start):
    per_device = shape[1] // (2 * SIDE)
    me = lax.axis_index("dp")
    core, my_x, my_y = me & 1, (me >> 1) & (SIDE - 1), me >> 3
    slot = lax.broadcasted_iota(jnp.int32, shape, 1) + start * SIDE * per_device
    piece = (slot * (65536 // per_device + 1)) >> 16
    first, second = offset(piece & (SIDE - 1), FIRST), offset(piece >> 2, SECOND)
    swapped = (first - second) * core
    x = (my_x + first - swapped) & (SIDE - 1)
    y = (my_y + second + swapped) & (SIDE - 1)
    column = ((y * SIDE + x) * 2 + core) * per_device + slot - piece * per_device
    return column >> 5


def split(value, terms):
    parts = []
    for _ in range(terms):
        part = value.astype(jnp.bfloat16)
        parts.append(part)
        value = value - part.astype(jnp.float32)
    return parts


def line_kernel(own, before, after, across, out):
    width = own.shape[0]
    for i, shard in enumerate((own, before, after, across)):
        out[i * width : (i + 1) * width, :] = shard[...]


def join(shards):
    width, depth = shards[0].shape
    return pl.pallas_call(
        line_kernel,
        out_shape=jax.ShapeDtypeStruct((len(shards) * width, depth), shards[0].dtype),
        in_specs=[VMEM] * len(shards),
        out_specs=VMEM,
        compiler_params=pltpu.CompilerParams(vmem_limit_bytes=1 << 20),
        name="line",
    )(*shards)


def turn_kernel(acts, grads, acts_out, grads_out):
    for rows, turned in ((acts, acts_out), (grads, grads_out)):
        for start in range(0, rows.shape[1], TOK_DEV):
            turned[start : start + TOK_DEV, :] = rows[:, start : start + TOK_DEV].T


def turn(acts, grads):
    return pl.pallas_call(
        turn_kernel,
        out_shape=tuple(jax.ShapeDtypeStruct(x.shape[::-1], x.dtype) for x in (acts, grads)),
        in_specs=[VMEM, VMEM],
        out_specs=(VMEM, VMEM),
        compiler_params=pltpu.CompilerParams(vmem_limit_bytes=2 << 20),
        cost_estimate=pl.CostEstimate(flops=0, bytes_accessed=6 << 20, transcendentals=0),
        name="turn",
    )(acts, grads)


def scores_kernel(acts, grads, w0, w1, grouping, *rest):
    *base, out, factors = rest
    width = w0.shape[0]
    factors[:width, :] = w0[...]
    factors[width:, :] = w1[...]
    dot = functools.partial(jnp.dot, preferred_element_type=jnp.float32)
    product = dot(factors[:, :MODEL], acts[...]) * dot(factors[:, MODEL:], grads[...])
    high, low = split(product, 2)
    scores = dot(grouping[...], high) + dot(grouping[...], low)
    out[...] = scores + base[0][...] if base else scores


def row_scores(acts, grads, pieces, grouping, *base):
    rows = acts.shape[1]
    slots = 2 * pieces[0].shape[0]
    return pl.pallas_call(
        scores_kernel,
        out_shape=jax.ShapeDtypeStruct((QUERIES, rows), jnp.float32),
        in_specs=[VMEM] * (5 + len(base)),
        out_specs=VMEM,
        scratch_shapes=[pltpu.VMEM((slots, MODEL + MOE_FF), jnp.bfloat16)],
        compiler_params=pltpu.CompilerParams(vmem_limit_bytes=4 << 20),
        cost_estimate=pl.CostEstimate(
            flops=2 * rows * slots * (MODEL + MOE_FF), bytes_accessed=7 << 20, transcendentals=0
        ),
        name="late_scores" if base else "early_scores",
    )(acts, grads, *pieces, grouping, *base)


def owners_kernel(tokens, norms, onehot, dense, early, late):
    for i, grouping in enumerate((early, late)):
        queries = slot_queries(grouping.shape, 2 * i)
        query_ids = lax.broadcasted_iota(jnp.int32, grouping.shape, 0)
        grouping[...] = (query_ids == queries).astype(jnp.float32).astype(jnp.bfloat16)
    rows = tokens.shape[1]
    token = jnp.broadcast_to(tokens[...], (HALF, rows)).T
    owner = lax.broadcasted_iota(jnp.int32, (rows, HALF), 1)
    for start in range(0, onehot.shape[1], HALF):
        hot = (token == owner + start).astype(jnp.float32).astype(jnp.bfloat16)
        onehot[:, start : start + HALF] = hot
    row = lax.broadcasted_iota(jnp.int32, (8, rows), 0)
    high, middle, low = split(norms[...], 3)
    terms = jnp.where(row == 0, high, jnp.where(row == 1, middle, low))
    part = jnp.dot(terms, onehot[...], preferred_element_type=jnp.float32)
    dense[...] = part[:1] + part[1:2] + part[2:3]


def owners(tokens, norms, shard_tokens, slots):
    rows = tokens.shape[1]
    return pl.pallas_call(
        owners_kernel,
        out_shape=(
            jax.ShapeDtypeStruct((rows, shard_tokens), jnp.bfloat16),
            jax.ShapeDtypeStruct((1, shard_tokens), jnp.float32),
            jax.ShapeDtypeStruct((QUERIES, slots // 2), jnp.bfloat16),
            jax.ShapeDtypeStruct((QUERIES, slots // 2), jnp.bfloat16),
        ),
        in_specs=[VMEM] * 2,
        out_specs=(VMEM,) * 4,
        compiler_params=pltpu.CompilerParams(vmem_limit_bytes=3 << 20),
        cost_estimate=pl.CostEstimate(
            flops=2 * rows * shard_tokens * 128, bytes_accessed=8 << 20, transcendentals=0
        ),
        name="owners",
    )(tokens, norms)


def scatter_kernel(mine, theirs, onehot, dense_norm, *rest):
    *outs, dense = rest
    table = jnp.concatenate(split(mine[...] + theirs[...], 3), 0)
    part = jnp.dot(table, onehot[...], preferred_element_type=jnp.float32)
    part = part[:QUERIES] + part[QUERIES : 2 * QUERIES] + part[2 * QUERIES :]
    experts = dense.shape[0]
    for i in range(experts):
        for half in range(2):
            start = i * TOK_DEV + half * HALF
            owned = slice(start, start + HALF)
            dense[i, half * QUERIES : (half + 1) * QUERIES, :] = part[:, owned]
            dense[i, 2 * QUERIES + half : 2 * QUERIES + half + 1, :] = dense_norm[:, owned]
    pair = lax.axis_index("expert") >> 1
    for out, step in zip(outs, (0, *STEPS)):
        first = ((pair + step) & (experts // 2 - 1)) * 2
        out[...] = dense[pl.ds(first, 2)]


def scatter(mine, theirs, onehot, dense_norm):
    block = (2 * QUERIES + 2, HALF)
    experts = onehot.shape[1] // TOK_DEV
    return pl.pallas_call(
        scatter_kernel,
        out_shape=(jax.ShapeDtypeStruct((2, *block), jnp.float32),) * (1 + len(STEPS)),
        in_specs=[VMEM] * 4,
        out_specs=(VMEM,) * (1 + len(STEPS)),
        scratch_shapes=[pltpu.VMEM((experts, *block), jnp.float32)],
        compiler_params=pltpu.CompilerParams(vmem_limit_bytes=2 << 20),
        name="scatter",
    )(mine, theirs, onehot, dense_norm)


def combine_kernel(own, *rest):
    *others, keep, give, total = rest
    total[...] = own[...]
    for other in others:
        total[...] += other[...]
    parity = lax.axis_index("expert") & 1
    keep[...] = total[parity]
    give[...] = total[1 - parity]


def combine(blocks):
    shape = blocks[0].shape
    return pl.pallas_call(
        combine_kernel,
        out_shape=(jax.ShapeDtypeStruct(shape[1:], jnp.float32),) * 2,
        in_specs=[VMEM] * len(blocks),
        out_specs=(VMEM, VMEM),
        scratch_shapes=[pltpu.VMEM(shape, jnp.float32)],
        compiler_params=pltpu.CompilerParams(vmem_limit_bytes=1 << 20),
        name="combine",
    )(*blocks)


def exchange(blocks, experts):
    parts = [blocks[0]]
    for block, step in zip(blocks[1:], STEPS):
        table = [(z, (z + 2 * step) % experts) for z in range(experts)]
        parts.append(lax.ppermute(block, "expert", table))
    keep, give = combine(parts)
    return keep + lax.ppermute(give, "expert", [(z, z ^ 1) for z in range(experts)])


def local(row_acts, row_grads, grad_factor, value_factor, counts, row_token):
    acts, grads = row_acts[0], row_grads[0]
    experts = lax.axis_size("expert")
    shard = jnp.concatenate([value_factor[0].T, grad_factor[0].T], 1)
    line = [shard] + [send(shard, first_axis(-d)) for d in FIRST[1:]]
    their_acts, their_grads = send(acts, SIBLING), send(grads, SIBLING)
    acts_norm = jnp.sum(jnp.square(acts.astype(jnp.float32)), 1)
    line[-1], acts_norm = lax.optimization_barrier((line[-1], acts_norm))
    line = join(line)
    line, acts, grads = lax.optimization_barrier((line, acts, grads))
    pieces = [line] + [send(line, second_axis(-d)) for d in SECOND[1:]]
    slots = acts.shape[0]
    live = lax.broadcasted_iota(jnp.int32, (1, slots), 1) < counts[0, 0]
    norms = acts_norm * jnp.sum(jnp.square(grads.astype(jnp.float32)), 1)
    their_rows = turn(their_acts, their_grads)
    my_rows = turn(acts, grads)
    norms, *their_rows = lax.optimization_barrier((norms, *their_rows))
    onehot, dense_norm, early, late = owners(
        jnp.where(live, row_token, -1),
        norms[None, :],
        TOK_DEV * experts,
        SIDE * SIDE * shard.shape[0],
    )
    for_them = row_scores(*their_rows, pieces[:2], early)
    mine = row_scores(*my_rows, pieces[:2], early)
    for_them, mine = lax.optimization_barrier((for_them, mine))
    for_them = row_scores(*their_rows, pieces[2:], late, for_them)
    theirs = send(for_them, SIBLING)
    mine = row_scores(*my_rows, pieces[2:], late, mine)
    summed = exchange(scatter(mine, theirs, onehot, dense_norm), experts)
    totals, norm_sum = summed[: 2 * QUERIES].reshape(2, QUERIES, HALF), summed[2 * QUERIES :]
    factor = lax.rsqrt(norm_sum / (MODEL * MOE_FF) + epsilon) / jnp.sqrt(jnp.float32(RANK))
    return (totals * factor[:, None, :]).transpose(0, 2, 1).reshape(TOK_DEV, QUERIES)


def solution(mesh):
    return jax.shard_map(
        local,
        mesh=mesh,
        in_specs=(
            P("expert", "dp", None),
            P("expert", "dp", None),
            P("expert", None, "dp"),
            P("expert", None, "dp"),
            P("expert", "dp"),
            P("expert", "dp"),
        ),
        out_specs=P(("expert", "dp"), None),
        check_vma=False,
    )
```

```python
import functools

import jax
import jax.numpy as jnp
from jax import lax
from jax.experimental import pallas as pl
from jax.experimental.pallas import tpu as pltpu
from jax.sharding import PartitionSpec as P

MODEL = 2048
MOE_FF = 768
RANK = 32
QUERIES = 24
TOK_DEV = 256
SIDE = 4
FIRST = (0, -1, 1, 2)
SECOND = (0, 2, -1, 1)
STEPS = (3, 2, 1)
HALF = TOK_DEV // 2

epsilon = 1e-06

VMEM = pl.BlockSpec(memory_space=pltpu.VMEM)
SMEM = pl.BlockSpec(memory_space=pltpu.SMEM)


def place(y, x, core):
    return ((y % SIDE) * SIDE + x % SIDE) * 2 + core


def pairs(step):
    return [
        (place(y, x, core), place(*step(y, x, core)))
        for y in range(SIDE)
        for x in range(SIDE)
        for core in range(2)
    ]


def first_axis(shift):
    return pairs(lambda y, x, core: (y, x + shift, 0) if core == 0 else (y + shift, x, 1))


def second_axis(shift):
    return pairs(lambda y, x, core: (y + shift, x, 0) if core == 0 else (y, x + shift, 1))


SIBLING = pairs(lambda y, x, core: (y, x, 1 - core))


def send(value, table):
    return lax.ppermute(value, "dp", table)


def offset(index, table):
    value = jnp.full_like(index, table[-1])
    for i, shift in enumerate(table[:-1]):
        value = jnp.where(index == i, shift, value)
    return value


def slot_queries(shape, start):
    per_device = shape[1] // (2 * SIDE)
    me = lax.axis_index("dp")
    core, my_x, my_y = me & 1, (me >> 1) & (SIDE - 1), me >> 3
    slot = lax.broadcasted_iota(jnp.int32, shape, 1) + start * SIDE * per_device
    piece = (slot * (65536 // per_device + 1)) >> 16
    first, second = offset(piece & (SIDE - 1), FIRST), offset(piece >> 2, SECOND)
    swapped = (first - second) * core
    x = (my_x + first - swapped) & (SIDE - 1)
    y = (my_y + second + swapped) & (SIDE - 1)
    column = ((y * SIDE + x) * 2 + core) * per_device + slot - piece * per_device
    return column >> 5


def split(value, terms):
    parts = []
    for _ in range(terms):
        part = value.astype(jnp.bfloat16)
        parts.append(part)
        value = value - part.astype(jnp.float32)
    return parts


def line_kernel(own, before, after, across, out):
    width = own.shape[0]
    for i, shard in enumerate((own, before, after, across)):
        out[i * width : (i + 1) * width, :] = shard[...]


def join(shards):
    width, depth = shards[0].shape
    return pl.pallas_call(
        line_kernel,
        out_shape=jax.ShapeDtypeStruct((len(shards) * width, depth), shards[0].dtype),
        in_specs=[VMEM] * len(shards),
        out_specs=VMEM,
        compiler_params=pltpu.CompilerParams(vmem_limit_bytes=1 << 20),
        name="line",
    )(*shards)


def turn_kernel(acts, grads, acts_out, grads_out):
    for rows, turned in ((acts, acts_out), (grads, grads_out)):
        for start in range(0, rows.shape[1], TOK_DEV):
            turned[start : start + TOK_DEV, :] = rows[:, start : start + TOK_DEV].T


def turn(acts, grads):
    return pl.pallas_call(
        turn_kernel,
        out_shape=tuple(jax.ShapeDtypeStruct(x.shape[::-1], x.dtype) for x in (acts, grads)),
        in_specs=[VMEM, VMEM],
        out_specs=(VMEM, VMEM),
        compiler_params=pltpu.CompilerParams(vmem_limit_bytes=2 << 20),
        cost_estimate=pl.CostEstimate(flops=0, bytes_accessed=6 << 20, transcendentals=0),
        name="turn",
    )(acts, grads)


def scores_kernel(acts, grads, w0, w1, grouping, *rest):
    *base, out, factors = rest
    width = w0.shape[0]
    factors[:width, :] = w0[...]
    factors[width:, :] = w1[...]
    dot = functools.partial(jnp.dot, preferred_element_type=jnp.float32)
    product = dot(factors[:, :MODEL], acts[...]) * dot(factors[:, MODEL:], grads[...])
    high, low = split(product, 2)
    scores = dot(grouping[...], high) + dot(grouping[...], low)
    out[...] = scores + base[0][...] if base else scores


def row_scores(acts, grads, pieces, grouping, *base):
    rows = acts.shape[1]
    slots = 2 * pieces[0].shape[0]
    return pl.pallas_call(
        scores_kernel,
        out_shape=jax.ShapeDtypeStruct((QUERIES, rows), jnp.float32),
        in_specs=[VMEM] * (5 + len(base)),
        out_specs=VMEM,
        scratch_shapes=[pltpu.VMEM((slots, MODEL + MOE_FF), jnp.bfloat16)],
        compiler_params=pltpu.CompilerParams(vmem_limit_bytes=4 << 20),
        cost_estimate=pl.CostEstimate(
            flops=2 * rows * slots * (MODEL + MOE_FF), bytes_accessed=7 << 20, transcendentals=0
        ),
        name="late_scores" if base else "early_scores",
    )(acts, grads, *pieces, grouping, *base)


def owners_kernel(counts, tokens, norms, onehot, dense, early, late):
    for i, grouping in enumerate((early, late)):
        queries = slot_queries(grouping.shape, 2 * i)
        query_ids = lax.broadcasted_iota(jnp.int32, grouping.shape, 0)
        grouping[...] = (query_ids == queries).astype(jnp.float32).astype(jnp.bfloat16)
    rows = tokens.shape[1]
    live = lax.broadcasted_iota(jnp.int32, (1, rows), 1) < counts[0, 0]
    token = jnp.broadcast_to(jnp.where(live, tokens[...], -1), (HALF, rows)).T
    owner = lax.broadcasted_iota(jnp.int32, (rows, HALF), 1)
    for start in range(0, onehot.shape[1], HALF):
        hot = (token == owner + start).astype(jnp.float32).astype(jnp.bfloat16)
        onehot[:, start : start + HALF] = hot
    row = lax.broadcasted_iota(jnp.int32, (8, rows), 0)
    high, middle, low = split(norms[...], 3)
    terms = jnp.where(row == 0, high, jnp.where(row == 1, middle, low))
    part = jnp.dot(terms, onehot[...], preferred_element_type=jnp.float32)
    dense[...] = part[:1] + part[1:2] + part[2:3]


def owners(counts, tokens, norms, shard_tokens, slots):
    rows = tokens.shape[1]
    return pl.pallas_call(
        owners_kernel,
        out_shape=(
            jax.ShapeDtypeStruct((rows, shard_tokens), jnp.bfloat16),
            jax.ShapeDtypeStruct((1, shard_tokens), jnp.float32),
            jax.ShapeDtypeStruct((QUERIES, slots // 2), jnp.bfloat16),
            jax.ShapeDtypeStruct((QUERIES, slots // 2), jnp.bfloat16),
        ),
        in_specs=[SMEM, VMEM, VMEM],
        out_specs=(VMEM,) * 4,
        compiler_params=pltpu.CompilerParams(vmem_limit_bytes=3 << 20),
        cost_estimate=pl.CostEstimate(
            flops=2 * rows * shard_tokens * 128, bytes_accessed=8 << 20, transcendentals=0
        ),
        name="owners",
    )(counts, tokens, norms)


def scatter_kernel(mine, theirs, onehot, dense_norm, *rest):
    *outs, dense = rest
    table = jnp.concatenate(split(mine[...] + theirs[...], 3), 0)
    part = jnp.dot(table, onehot[...], preferred_element_type=jnp.float32)
    part = part[:QUERIES] + part[QUERIES : 2 * QUERIES] + part[2 * QUERIES :]
    experts = dense.shape[0]
    for i in range(experts):
        for half in range(2):
            start = i * TOK_DEV + half * HALF
            owned = slice(start, start + HALF)
            dense[i, half * QUERIES : (half + 1) * QUERIES, :] = part[:, owned]
            dense[i, 2 * QUERIES + half : 2 * QUERIES + half + 1, :] = dense_norm[:, owned]
    pair = lax.axis_index("expert") >> 1
    for out, step in zip(outs, (0, *STEPS)):
        first = ((pair + step) & (experts // 2 - 1)) * 2
        out[...] = dense[pl.ds(first, 2)]


def scatter(mine, theirs, onehot, dense_norm):
    block = (2 * QUERIES + 2, HALF)
    experts = onehot.shape[1] // TOK_DEV
    return pl.pallas_call(
        scatter_kernel,
        out_shape=(jax.ShapeDtypeStruct((2, *block), jnp.float32),) * (1 + len(STEPS)),
        in_specs=[VMEM] * 4,
        out_specs=(VMEM,) * (1 + len(STEPS)),
        scratch_shapes=[pltpu.VMEM((experts, *block), jnp.float32)],
        compiler_params=pltpu.CompilerParams(vmem_limit_bytes=2 << 20),
        name="scatter",
    )(mine, theirs, onehot, dense_norm)


def combine_kernel(own, *rest):
    *others, keep, give, total = rest
    total[...] = own[...]
    for other in others:
        total[...] += other[...]
    parity = lax.axis_index("expert") & 1
    keep[...] = total[parity]
    give[...] = total[1 - parity]


def combine(blocks):
    shape = blocks[0].shape
    return pl.pallas_call(
        combine_kernel,
        out_shape=(jax.ShapeDtypeStruct(shape[1:], jnp.float32),) * 2,
        in_specs=[VMEM] * len(blocks),
        out_specs=(VMEM, VMEM),
        scratch_shapes=[pltpu.VMEM(shape, jnp.float32)],
        compiler_params=pltpu.CompilerParams(vmem_limit_bytes=1 << 20),
        name="combine",
    )(*blocks)


def exchange(blocks, experts):
    parts = [blocks[0]]
    for block, step in zip(blocks[1:], STEPS):
        table = [(z, (z + 2 * step) % experts) for z in range(experts)]
        parts.append(lax.ppermute(block, "expert", table))
    keep, give = combine(parts)
    return keep + lax.ppermute(give, "expert", [(z, z ^ 1) for z in range(experts)])


def local(row_acts, row_grads, grad_factor, value_factor, counts, row_token):
    acts, grads = row_acts[0], row_grads[0]
    experts = lax.axis_size("expert")
    shard = jnp.concatenate([value_factor[0].T, grad_factor[0].T], 1)
    line = [shard] + [send(shard, first_axis(-d)) for d in FIRST[1:]]
    their_acts, their_grads = send(acts, SIBLING), send(grads, SIBLING)
    acts_norm = jnp.sum(jnp.square(acts.astype(jnp.float32)), 1)
    line[-1], acts_norm = lax.optimization_barrier((line[-1], acts_norm))
    line = join(line)
    line, acts, grads = lax.optimization_barrier((line, acts, grads))
    pieces = [line] + [send(line, second_axis(-d)) for d in SECOND[1:]]
    norms = acts_norm * jnp.sum(jnp.square(grads.astype(jnp.float32)), 1)
    their_rows = turn(their_acts, their_grads)
    my_rows = turn(acts, grads)
    norms, *their_rows = lax.optimization_barrier((norms, *their_rows))
    onehot, dense_norm, early, late = owners(
        counts,
        row_token,
        norms[None, :],
        TOK_DEV * experts,
        SIDE * SIDE * shard.shape[0],
    )
    for_them = row_scores(*their_rows, pieces[:2], early)
    mine = row_scores(*my_rows, pieces[:2], early)
    for_them, mine = lax.optimization_barrier((for_them, mine))
    for_them = row_scores(*their_rows, pieces[2:], late, for_them)
    theirs = send(for_them, SIBLING)
    mine = row_scores(*my_rows, pieces[2:], late, mine)
    summed = exchange(scatter(mine, theirs, onehot, dense_norm), experts)
    totals, norm_sum = summed[: 2 * QUERIES].reshape(2, QUERIES, HALF), summed[2 * QUERIES :]
    factor = lax.rsqrt(norm_sum / (MODEL * MOE_FF) + epsilon) / jnp.sqrt(jnp.float32(RANK))
    return (totals * factor[:, None, :]).transpose(0, 2, 1).reshape(TOK_DEV, QUERIES)


def solution(mesh):
    return jax.shard_map(
        local,
        mesh=mesh,
        in_specs=(
            P("expert", "dp", None),
            P("expert", "dp", None),
            P("expert", None, "dp"),
            P("expert", None, "dp"),
            P("expert", "dp"),
            P("expert", "dp"),
        ),
        out_specs=P(("expert", "dp"), None),
        check_vma=False,
    )
```

```python
import functools

import jax
import jax.numpy as jnp
from jax import lax
from jax.experimental import pallas as pl
from jax.experimental.pallas import tpu as pltpu
from jax.sharding import PartitionSpec as P

MODEL = 2048
MOE_FF = 768
RANK = 32
QUERIES = 24
TOK_DEV = 256
SIDE = 4
FIRST = (0, -1, 1, 2)
SECOND = (0, 2, -1, 1)
STEPS = (3, 2, 1)
HALF = TOK_DEV // 2

epsilon = 1e-06

VMEM = pl.BlockSpec(memory_space=pltpu.VMEM)
SMEM = pl.BlockSpec(memory_space=pltpu.SMEM)


def place(y, x, core):
    return ((y % SIDE) * SIDE + x % SIDE) * 2 + core


def pairs(step):
    return [
        (place(y, x, core), place(*step(y, x, core)))
        for y in range(SIDE)
        for x in range(SIDE)
        for core in range(2)
    ]


def first_axis(shift):
    return pairs(lambda y, x, core: (y, x + shift, 0) if core == 0 else (y + shift, x, 1))


def second_axis(shift):
    return pairs(lambda y, x, core: (y + shift, x, 0) if core == 0 else (y, x + shift, 1))


SIBLING = pairs(lambda y, x, core: (y, x, 1 - core))


def send(value, table):
    return lax.ppermute(value, "dp", table)


def offset(index, table):
    value = jnp.full_like(index, table[-1])
    for i, shift in enumerate(table[:-1]):
        value = jnp.where(index == i, shift, value)
    return value


def slot_queries(shape, start):
    per_device = shape[1] // (2 * SIDE)
    me = lax.axis_index("dp")
    core, my_x, my_y = me & 1, (me >> 1) & (SIDE - 1), me >> 3
    slot = lax.broadcasted_iota(jnp.int32, shape, 1) + start * SIDE * per_device
    piece = (slot * (65536 // per_device + 1)) >> 16
    first, second = offset(piece & (SIDE - 1), FIRST), offset(piece >> 2, SECOND)
    swapped = (first - second) * core
    x = (my_x + first - swapped) & (SIDE - 1)
    y = (my_y + second + swapped) & (SIDE - 1)
    column = ((y * SIDE + x) * 2 + core) * per_device + slot - piece * per_device
    return column >> 5


def split(value, terms):
    parts = []
    for _ in range(terms):
        part = value.astype(jnp.bfloat16)
        parts.append(part)
        value = value - part.astype(jnp.float32)
    return parts


def line_kernel(own, before, after, across, out):
    width = own.shape[0]
    for i, shard in enumerate((own, before, after, across)):
        out[i * width : (i + 1) * width, :] = shard[...]


def join(shards):
    width, depth = shards[0].shape
    return pl.pallas_call(
        line_kernel,
        out_shape=jax.ShapeDtypeStruct((len(shards) * width, depth), shards[0].dtype),
        in_specs=[VMEM] * len(shards),
        out_specs=VMEM,
        compiler_params=pltpu.CompilerParams(vmem_limit_bytes=1 << 20),
        name="line",
    )(*shards)


def turn_kernel(rows, turned):
    for start in range(0, rows.shape[1], TOK_DEV):
        turned[start : start + TOK_DEV, :] = rows[:, start : start + TOK_DEV].T


def turn(rows):
    return pl.pallas_call(
        turn_kernel,
        out_shape=jax.ShapeDtypeStruct(rows.shape[::-1], rows.dtype),
        in_specs=[VMEM],
        out_specs=VMEM,
        compiler_params=pltpu.CompilerParams(vmem_limit_bytes=2 << 20),
        cost_estimate=pl.CostEstimate(
            flops=0, bytes_accessed=4 * rows.size, transcendentals=0
        ),
        name="turn",
    )(rows)


def scores_kernel(acts, grads, w0, w1, grouping, *rest):
    *base, out, factors = rest
    width = w0.shape[0]
    factors[:width, :] = w0[...]
    factors[width:, :] = w1[...]
    dot = functools.partial(jnp.dot, preferred_element_type=jnp.float32)
    product = dot(factors[:, :MODEL], acts[...]) * dot(factors[:, MODEL:], grads[...])
    high, low = split(product, 2)
    scores = dot(grouping[...], high) + dot(grouping[...], low)
    out[...] = scores + base[0][...] if base else scores


def row_scores(acts, grads, pieces, grouping, *base):
    rows = acts.shape[1]
    slots = 2 * pieces[0].shape[0]
    return pl.pallas_call(
        scores_kernel,
        out_shape=jax.ShapeDtypeStruct((QUERIES, rows), jnp.float32),
        in_specs=[VMEM] * (5 + len(base)),
        out_specs=VMEM,
        scratch_shapes=[pltpu.VMEM((slots, MODEL + MOE_FF), jnp.bfloat16)],
        compiler_params=pltpu.CompilerParams(vmem_limit_bytes=4 << 20),
        cost_estimate=pl.CostEstimate(
            flops=2 * rows * slots * (MODEL + MOE_FF), bytes_accessed=7 << 20, transcendentals=0
        ),
        name="late_scores" if base else "early_scores",
    )(acts, grads, *pieces, grouping, *base)


def owners_kernel(counts, tokens, norms, onehot, dense, early, late):
    for i, grouping in enumerate((early, late)):
        queries = slot_queries(grouping.shape, 2 * i)
        query_ids = lax.broadcasted_iota(jnp.int32, grouping.shape, 0)
        grouping[...] = (query_ids == queries).astype(jnp.float32).astype(jnp.bfloat16)
    rows = tokens.shape[1]
    live = lax.broadcasted_iota(jnp.int32, (1, rows), 1) < counts[0, 0]
    token = jnp.broadcast_to(jnp.where(live, tokens[...], -1), (HALF, rows)).T
    owner = lax.broadcasted_iota(jnp.int32, (rows, HALF), 1)
    for start in range(0, onehot.shape[1], HALF):
        hot = (token == owner + start).astype(jnp.float32).astype(jnp.bfloat16)
        onehot[:, start : start + HALF] = hot
    row = lax.broadcasted_iota(jnp.int32, (8, rows), 0)
    high, middle, low = split(norms[...], 3)
    terms = jnp.where(row == 0, high, jnp.where(row == 1, middle, low))
    part = jnp.dot(terms, onehot[...], preferred_element_type=jnp.float32)
    dense[...] = part[:1] + part[1:2] + part[2:3]


def owners(counts, tokens, norms, shard_tokens, slots):
    rows = tokens.shape[1]
    return pl.pallas_call(
        owners_kernel,
        out_shape=(
            jax.ShapeDtypeStruct((rows, shard_tokens), jnp.bfloat16),
            jax.ShapeDtypeStruct((1, shard_tokens), jnp.float32),
            jax.ShapeDtypeStruct((QUERIES, slots // 2), jnp.bfloat16),
            jax.ShapeDtypeStruct((QUERIES, slots // 2), jnp.bfloat16),
        ),
        in_specs=[SMEM, VMEM, VMEM],
        out_specs=(VMEM,) * 4,
        compiler_params=pltpu.CompilerParams(vmem_limit_bytes=3 << 20),
        cost_estimate=pl.CostEstimate(
            flops=2 * rows * shard_tokens * 128, bytes_accessed=8 << 20, transcendentals=0
        ),
        name="owners",
    )(counts, tokens, norms)


def scatter_kernel(mine, theirs, onehot, dense_norm, *rest):
    *outs, dense = rest
    table = jnp.concatenate(split(mine[...] + theirs[...], 3), 0)
    part = jnp.dot(table, onehot[...], preferred_element_type=jnp.float32)
    part = part[:QUERIES] + part[QUERIES : 2 * QUERIES] + part[2 * QUERIES :]
    experts = dense.shape[0]
    for i in range(experts):
        for half in range(2):
            start = i * TOK_DEV + half * HALF
            owned = slice(start, start + HALF)
            dense[i, half * QUERIES : (half + 1) * QUERIES, :] = part[:, owned]
            dense[i, 2 * QUERIES + half : 2 * QUERIES + half + 1, :] = dense_norm[:, owned]
    pair = lax.axis_index("expert") >> 1
    for out, step in zip(outs, (0, *STEPS)):
        first = ((pair + step) & (experts // 2 - 1)) * 2
        out[...] = dense[pl.ds(first, 2)]


def scatter(mine, theirs, onehot, dense_norm):
    block = (2 * QUERIES + 2, HALF)
    experts = onehot.shape[1] // TOK_DEV
    return pl.pallas_call(
        scatter_kernel,
        out_shape=(jax.ShapeDtypeStruct((2, *block), jnp.float32),) * (1 + len(STEPS)),
        in_specs=[VMEM] * 4,
        out_specs=(VMEM,) * (1 + len(STEPS)),
        scratch_shapes=[pltpu.VMEM((experts, *block), jnp.float32)],
        compiler_params=pltpu.CompilerParams(vmem_limit_bytes=2 << 20),
        name="scatter",
    )(mine, theirs, onehot, dense_norm)


def combine_kernel(own, *rest):
    *others, keep, give, total = rest
    total[...] = own[...]
    for other in others:
        total[...] += other[...]
    parity = lax.axis_index("expert") & 1
    keep[...] = total[parity]
    give[...] = total[1 - parity]


def combine(blocks):
    shape = blocks[0].shape
    return pl.pallas_call(
        combine_kernel,
        out_shape=(jax.ShapeDtypeStruct(shape[1:], jnp.float32),) * 2,
        in_specs=[VMEM] * len(blocks),
        out_specs=(VMEM, VMEM),
        scratch_shapes=[pltpu.VMEM(shape, jnp.float32)],
        compiler_params=pltpu.CompilerParams(vmem_limit_bytes=1 << 20),
        name="combine",
    )(*blocks)


def exchange(blocks, experts):
    parts = [blocks[0]]
    for block, step in zip(blocks[1:], STEPS):
        table = [(z, (z + 2 * step) % experts) for z in range(experts)]
        parts.append(lax.ppermute(block, "expert", table))
    keep, give = combine(parts)
    return keep + lax.ppermute(give, "expert", [(z, z ^ 1) for z in range(experts)])


def local(row_acts, row_grads, grad_factor, value_factor, counts, row_token):
    acts, grads = row_acts[0], row_grads[0]
    experts = lax.axis_size("expert")
    shard = jnp.concatenate([value_factor[0].T, grad_factor[0].T], 1)
    line = [shard] + [send(shard, first_axis(-d)) for d in FIRST[1:]]
    their_acts, their_grads = send(acts, SIBLING), send(grads, SIBLING)
    acts_norm = jnp.sum(jnp.square(acts.astype(jnp.float32)), 1)
    line[-1], acts_norm = lax.optimization_barrier((line[-1], acts_norm))
    line = join(line)
    line, acts, grads = lax.optimization_barrier((line, acts, grads))
    pieces = [line] + [send(line, second_axis(-d)) for d in SECOND[1:]]
    norms = acts_norm * jnp.sum(jnp.square(grads.astype(jnp.float32)), 1)
    their_rows = turn(their_acts), turn(their_grads)
    my_rows = turn(acts), turn(grads)
    norms, *their_rows = lax.optimization_barrier((norms, *their_rows))
    onehot, dense_norm, early, late = owners(
        counts,
        row_token,
        norms[None, :],
        TOK_DEV * experts,
        SIDE * SIDE * shard.shape[0],
    )
    for_them = row_scores(*their_rows, pieces[:2], early)
    mine = row_scores(*my_rows, pieces[:2], early)
    for_them, mine = lax.optimization_barrier((for_them, mine))
    for_them = row_scores(*their_rows, pieces[2:], late, for_them)
    theirs = send(for_them, SIBLING)
    mine = row_scores(*my_rows, pieces[2:], late, mine)
    summed = exchange(scatter(mine, theirs, onehot, dense_norm), experts)
    totals, norm_sum = summed[: 2 * QUERIES].reshape(2, QUERIES, HALF), summed[2 * QUERIES :]
    factor = lax.rsqrt(norm_sum / (MODEL * MOE_FF) + epsilon) / jnp.sqrt(jnp.float32(RANK))
    return (totals * factor[:, None, :]).transpose(0, 2, 1).reshape(TOK_DEV, QUERIES)


def solution(mesh):
    return jax.shard_map(
        local,
        mesh=mesh,
        in_specs=(
            P("expert", "dp", None),
            P("expert", "dp", None),
            P("expert", None, "dp"),
            P("expert", None, "dp"),
            P("expert", "dp"),
            P("expert", "dp"),
        ),
        out_specs=P(("expert", "dp"), None),
        check_vma=False,
    )
```
